256 devices in a mesh: seq: 16 (over z, core), head: 16 (over x, y).
Axes of the slice: x: 4, y: 4, z: 8, core: 2. Of those that a mesh axis runs over, the one named last changes fastest.
Arguments:
- queries: bfloat16 [4096, 16384], P('seq', 'head'), may hold values from -8 to 8
- keys: bfloat16 [4096, 1024], P('seq'), may hold values from -8 to 8
- values: bfloat16 [4096, 1024], P('seq'), may hold values from -8 to 8
- query_map: bfloat16 [128, 128, 128], P('head'), may hold values from -3 to 3
- key_map: bfloat16 [8, 128, 128], replicated, may hold values from -3 to 3
- positions: int32 [4096], P('seq'), may hold values from 0 to 131071, as said below
Outputs:
- error_grad: bfloat16 [4096, 16384], P('seq', 'head')
The draws below stay inside these ranges and needn't reach their ends.
Inputs may be any that keep to these rules, and one draw needn't show every extreme that they name: `positions`: each token's position is one more than the token before it, or 0 where a new document begins; the window begins inside a document that ends at position 131071, and at least one document begins inside the window.
All inputs are finite; a program needn't handle non-finite values.
Results may differ from the reference program's by a relative error of at most 0.0085.
Values may be sent and summed in bfloat16 or wider, within the bound.
No kernel may reach another device: no remote copies, remote signals or barrier semaphores. Data moves between devices by JAX's collectives and lax.ppermute only.
A program may use at most 64 MiB of HBM per device.

```python
import math
import jax
import jax.numpy as jnp
from jax import lax

HD = 128
QHEADS = 128
KVH = 8
LENGTH = 131072
SEQ = 4096


feature_shift = 3.0


feature_spread = 2.0


def common_plan(key):
    folded_key = jax.random.fold_in(key, 5151)
    key_one, key_two = jax.random.split(folded_key)
    key_signs = (jax.random.randint(key_one, (KVH, HD), 0, 2) * 2 - 1).astype(jnp.float32)
    query_signs = (jax.random.randint(key_two, (QHEADS, HD), 0, 2) * 2 - 1).astype(jnp.float32)
    return (key_signs, query_signs)


def structured_map(key, signs):
    count = signs.shape[0]
    gaussian = jax.random.normal(key, (count, HD, HD), jnp.float32)
    orthogonal, unused = jnp.linalg.qr(gaussian)
    projector = jnp.eye(HD, dtype=jnp.float32)[None] - signs[:, :, None] * signs[:, None, :] / HD
    rotated = jnp.einsum('gij,gjk->gik', projector, orthogonal, precision=lax.Precision.HIGHEST)
    shifted = feature_shift / HD * signs[:, :, None] * jnp.ones((1, 1, HD), jnp.float32)
    return feature_spread * rotated - shifted


def base_keys(key):
    full_shape = (SEQ, KVH * HD)
    own_key = jax.random.fold_in(key, 17)
    key_signs, query_signs = common_plan(key)
    noise = jnp.clip(jax.random.normal(own_key, full_shape, jnp.float32), -6.0, 6.0)
    return noise + key_signs.reshape(1, KVH * HD)


def draw_queries(key, part):
    full_shape = (SEQ, QHEADS * HD)
    key_signs, query_signs = common_plan(key)
    drawn = jnp.clip(jax.random.normal(key, full_shape, jnp.float32), -6.0, 6.0) + query_signs.reshape(1, QHEADS * HD)
    return drawn.astype(jnp.bfloat16)


def draw_keys(key, part):
    drawn = base_keys(key)
    return drawn.astype(jnp.bfloat16)


def draw_values(key, part):
    keys_base = base_keys(key)
    key_signs, query_signs = common_plan(key)
    key_maps = structured_map(jax.random.fold_in(key, 31), key_signs)
    projected = jnp.einsum('tgd,gde->tge', keys_base.reshape(SEQ, KVH, HD), key_maps, precision=lax.Precision.HIGHEST)
    noise_key = jax.random.fold_in(key, 53)
    noise = 0.5 * jax.random.normal(noise_key, (SEQ, KVH, HD), jnp.float32)
    drawn = (projected + feature_shift) / feature_spread + noise
    return jnp.clip(drawn, -8.0, 8.0).reshape(SEQ, KVH * HD).astype(jnp.bfloat16)


def draw_key_map(key, part):
    key_signs, query_signs = common_plan(key)
    return structured_map(jax.random.fold_in(key, 31), key_signs).astype(jnp.bfloat16)


def draw_query_map(key, part):
    key_signs, query_signs = common_plan(key)
    return structured_map(jax.random.fold_in(key, 37), query_signs).astype(jnp.bfloat16)


def draw_positions(key, part):
    key_break, key_first = jax.random.split(jax.random.fold_in(key, 99))
    token_order = jnp.arange(SEQ, dtype=jnp.int32)
    first_break = jax.random.randint(key_first, (), 1, SEQ)
    random_breaks = jax.random.randint(key_break, (SEQ,), 0, 1024) == 0
    breaks = random_breaks & (token_order > first_break) | (token_order == first_break)
    latest = lax.cummax(jnp.where(breaks, token_order, 0), axis=0)
    return jnp.where(token_order < first_break, LENGTH - first_break + token_order, token_order - latest).astype(jnp.int32)


def setup_inputs(seed: int = 0) -> dict:
    seeds = jax.random.split(jax.random.key(seed), 7)
    queries = draw_queries(jax.random.fold_in(seeds[6], 71), 0)
    keys = draw_keys(jax.random.fold_in(seeds[6], 71), 0)
    values = draw_values(jax.random.fold_in(seeds[6], 71), 0)
    query_map = draw_query_map(jax.random.fold_in(seeds[6], 71), 0)
    key_map = draw_key_map(jax.random.fold_in(seeds[6], 71), 0)
    positions = draw_positions(jax.random.fold_in(seeds[6], 71), 0)
    return dict(queries=queries, keys=keys, values=values, query_map=query_map, key_map=key_map, positions=positions)


epsilon = 1e-06
masked_score = -1e+30
highest = lax.Precision.HIGHEST

def reference(queries, keys, values, query_map, key_map, positions):
    group_size = QHEADS // KVH
    angles = 0.5 * math.pi / LENGTH * positions.astype(jnp.float32)
    cosine_part = jnp.cos(angles)[:, None]
    sine_part = jnp.sin(angles)[:, None]
    token_order = jnp.arange(SEQ, dtype=jnp.int32)
    causal = token_order[:, None] >= token_order[None, :]
    scaling = 1.0 / math.sqrt(HD)
    block_rows = math.gcd(512, SEQ)
    blocks = SEQ // block_rows
    inside = jnp.arange(block_rows)[:, None] >= jnp.arange(block_rows)[None, :]

    def key_features(group_index):
        group_keys = lax.dynamic_slice_in_dim(keys, group_index * HD, HD, 1)
        mapped = jax.nn.elu(jnp.dot(group_keys.astype(jnp.float32), key_map[group_index].astype(jnp.float32), preferred_element_type=jnp.float32)) + 1.0
        return jnp.concatenate([cosine_part * mapped, sine_part * mapped], axis=1).astype(jnp.bfloat16)
    key_feats = lax.map(key_features, jnp.arange(KVH, dtype=jnp.int32))

    def one_head(head_index):
        group_index = head_index // group_size
        head_queries = lax.dynamic_slice_in_dim(queries, head_index * HD, HD, 1)
        head_keys = lax.dynamic_slice_in_dim(keys, group_index * HD, HD, 1)
        head_values = lax.dynamic_slice_in_dim(values, group_index * HD, HD, 1)
        scores = jnp.dot(head_queries.astype(jnp.float32), head_keys.T.astype(jnp.float32), preferred_element_type=jnp.float32) * scaling
        scores = jnp.where(causal, scores, masked_score)
        largest = lax.optimization_barrier(jnp.max(scores, axis=1, keepdims=True))
        weights = jnp.where(causal, jnp.exp(scores - largest), 0.0)
        weight_total = lax.optimization_barrier(jnp.sum(weights, axis=1, keepdims=True))
        teacher = (jnp.dot(weights.astype(jnp.bfloat16).astype(jnp.float32), head_values.astype(jnp.float32), preferred_element_type=jnp.float32) / weight_total).astype(jnp.bfloat16)
        mapped = jax.nn.elu(jnp.dot(head_queries.astype(jnp.float32), query_map[head_index].astype(jnp.float32), preferred_element_type=jnp.float32)) + 1.0
        query_feats = jnp.concatenate([cosine_part * mapped, sine_part * mapped], axis=1).astype(jnp.bfloat16)
        query_rows = query_feats.astype(jnp.float32).reshape(blocks, block_rows, 2 * HD)
        group_feats = key_feats[group_index].astype(jnp.float32).reshape(blocks, block_rows, 2 * HD)
        value_rows = head_values.astype(jnp.float32).reshape(blocks, block_rows, HD)
        totals = jnp.einsum('bjf,bjd->bfd', group_feats, value_rows, precision=highest)
        masses = lax.optimization_barrier(jnp.sum(group_feats, axis=1))
        before = jnp.concatenate([jnp.zeros((1, 2 * HD, HD), jnp.float32), jnp.cumsum(totals, axis=0)[:-1]], axis=0)
        mass_before = jnp.concatenate([jnp.zeros((1, 2 * HD), jnp.float32), jnp.cumsum(masses, axis=0)[:-1]], axis=0)
        inner_block = jnp.where(inside, jnp.einsum('bif,bjf->bij', query_rows, group_feats, precision=highest), 0.0)
        numerator = jnp.einsum('bij,bjd->bid', inner_block, value_rows, precision=highest) + jnp.einsum('bif,bfd->bid', query_rows, before, precision=highest)
        denominator = lax.optimization_barrier(jnp.sum(inner_block, axis=2)) + jnp.einsum('bif,bf->bi', query_rows, mass_before, precision=highest)
        student = (numerator / (denominator[..., None] + epsilon)).reshape(SEQ, HD)
        return (2.0 * (student - teacher.astype(jnp.float32))).astype(jnp.bfloat16)
    gradient = lax.map(one_head, jnp.arange(QHEADS, dtype=jnp.int32))
    return jnp.transpose(gradient, (1, 0, 2)).reshape(SEQ, QHEADS * HD)
```

```python
import math

import jax
import jax.numpy as jnp
from jax import lax
from jax.experimental import pallas as pl
from jax.experimental.pallas import tpu as pltpu
from jax.sharding import Mesh
from jax.sharding import PartitionSpec as P

QHEADS = 128
KVH = 8
LENGTH = 131072
HD = 128
ROWS = 272
TOK = 256
epsilon = 1e-06
masked_score = -1e30
to_exp2 = math.log2(math.e) / math.sqrt(HD)

SWAP = [(0, 1), (1, 0)]


def ring(shift):
    return [(i, (i + shift) % 8) for i in range(8)]


def call(kernel, out_shape, scratch=(), flops=0, nbytes=0, transcendentals=0, name=None):
    return pl.pallas_call(
        kernel,
        out_shape=out_shape,
        scratch_shapes=list(scratch),
        name=name,
        compiler_params=pltpu.CompilerParams(vmem_limit_bytes=40 * 1024 * 1024),
        cost_estimate=pl.CostEstimate(
            flops=flops, bytes_accessed=nbytes, transcendentals=transcendentals
        ),
    )


def first_group(local_heads):
    return lax.axis_index("head") * local_heads // (QHEADS // KVH)


def pack_kernel(keys_ref, values_ref, pos_ref, out_ref, sems):
    g = pl.multiple_of(first_group(8) * HD, HD)
    ck = pltpu.make_async_copy(keys_ref.at[:, pl.ds(g, HD)], out_ref.at[0:TOK, 0:HD], sems.at[0])
    cv = pltpu.make_async_copy(
        values_ref.at[:, pl.ds(g, HD)], out_ref.at[0:TOK, HD : 2 * HD], sems.at[1]
    )
    ck.start()
    cv.start()
    p = pos_ref[...]
    row = lax.broadcasted_iota(jnp.int32, (16, TOK), 0)
    digit = jnp.where(row == 0, p & 255, jnp.where(row == 1, (p >> 8) & 255, p >> 16))
    digit = jnp.where(row < 3, digit, 0)
    out_ref[TOK:ROWS, :] = digit.astype(jnp.float32).astype(jnp.bfloat16)
    ck.wait()
    cv.wait()


def angles_of(block_ref, base=0):
    d = block_ref[base + TOK : base + ROWS, :].astype(jnp.float32)
    p = d[0:1, :] + 256.0 * d[1:2, :] + 65536.0 * d[2:3, :]
    a = (0.5 * math.pi / LENGTH) * p
    return jnp.cos(a), jnp.sin(a)


def elu1(x):
    return jnp.where(x > 0.0, x + 1.0, jnp.exp(jnp.minimum(x, 0.0)))


def dot(a, b, dims):
    return lax.dot_general(a, b, (dims, ((), ())), preferred_element_type=jnp.float32)


def nn(a, b):
    return dot(a, b, ((1,), (0,)))


def nt(a, b):
    return dot(a, b, ((1,), (1,)))


def key_feats_t(block_ref, key_map):
    c, s = angles_of(block_ref)
    phi = elu1(dot(key_map, block_ref[0:TOK, 0:HD], ((0,), (1,))))
    return jnp.concatenate([c * phi, s * phi], axis=0).astype(jnp.bfloat16)


def with_ones(v):
    return jnp.concatenate([v, jnp.ones(v.shape, v.dtype)], axis=1)


def local_kernel(own_ref, q_ref, qmap_ref, kmap_ref, qf_ref, m_ref, accl_ref, stu_ref):
    k = own_ref[0:TOK, 0:HD]
    va = with_ones(own_ref[0:TOK, HD : 2 * HD])
    c, s = angles_of(own_ref)
    ct = jnp.broadcast_to(c, (HD, TOK)).T
    st = jnp.broadcast_to(s, (HD, TOK)).T
    kft = key_feats_t(own_ref, kmap_ref[first_group(8)])
    causal = lax.broadcasted_iota(jnp.int32, (TOK, TOK), 0) >= lax.broadcasted_iota(
        jnp.int32, (TOK, TOK), 1
    )
    for h in range(8):
        q = q_ref[:, h * HD : (h + 1) * HD]
        phi = elu1(nn(q, qmap_ref[h]))
        qf = jnp.concatenate([ct * phi, st * phi], axis=1).astype(jnp.bfloat16)
        qf_ref[h] = qf
        inner = jnp.where(causal, nn(qf, kft), 0.0).astype(jnp.bfloat16)
        stu_ref[h] = nn(inner, va)
        x = jnp.where(causal, nt(q, k), masked_score)
        m = jnp.max(x, axis=1, keepdims=True)
        p = jnp.exp2((x - m) * to_exp2).astype(jnp.bfloat16)
        accl_ref[h] = nn(p, va)
        m_ref[h] = jnp.broadcast_to(m, (TOK, HD))


def absorb(block_refs, q_ref, m_ref, accl_ref):
    for h in range(8):
        q = q_ref[:, h * HD : (h + 1) * HD]
        xs = [nt(q, b[0:TOK, 0:HD]) for b in block_refs]
        m0 = m_ref[h]
        top = jnp.max(xs[0], axis=1, keepdims=True)
        for x in xs[1:]:
            top = jnp.maximum(top, jnp.max(x, axis=1, keepdims=True))
        m1 = jnp.maximum(m0, jnp.broadcast_to(top, m0.shape))
        f = jnp.exp2((m0 - m1) * to_exp2)
        acc = accl_ref[h] * jnp.concatenate([f, f], axis=1)
        mm = jnp.concatenate([m1, m1], axis=1)
        for x, b in zip(xs, block_refs):
            p = jnp.exp2((x - mm) * to_exp2).astype(jnp.bfloat16)
            acc = acc + nn(p, with_ones(b[0:TOK, HD : 2 * HD]))
        accl_ref[h] = acc
        m_ref[h] = m1


def gather_state(block_refs, kmap_ref, state_ref):
    km = kmap_ref[first_group(8)]
    add = None
    for b in block_refs:
        part = nn(key_feats_t(b, km), with_ones(b[0:TOK, HD : 2 * HD]))
        add = part if add is None else add + part
    state_ref[...] += add


def validity():
    z = lax.axis_index("z")
    return {
        "u": lambda k: z >= k,
        "d": lambda k: z >= 8 - k,
        "x": z >= 4,
    }


def mid_kernel(pb, u1, u1s, d1, d1s, x, xs, u2, u2s, d2, d2s, q_ref, kmap_ref, m_in, accl_in,
               m_ref, accl_ref, state_ref):
    m_ref[...] = m_in[...]
    accl_ref[...] = accl_in[...]
    state_ref[...] = jnp.zeros_like(state_ref)
    ok = validity()

    def take(when, *blocks):
        @pl.when(when)
        def _():
            gather_state(blocks, kmap_ref, state_ref)
            absorb(blocks, q_ref, m_ref, accl_ref)

    take(lax.axis_index("c") == 1, pb)
    take(ok["u"](1), u1, u1s)
    take(ok["d"](1), d1, d1s)
    take(ok["x"], x, xs)
    take(ok["u"](2), u2, u2s)
    take(ok["d"](2), d2, d2s)


def last_kernel(u3, u3s, d3, d3s, q_ref, kmap_ref, qf_ref, stu_ref, m_in, accl_in, state_in,
                out_ref, m_ref, accl_ref, state_ref):
    m_ref[...] = m_in[...]
    accl_ref[...] = accl_in[...]
    state_ref[...] = state_in[...]
    ok = validity()

    def take(when, *blocks):
        @pl.when(when)
        def _():
            gather_state(blocks, kmap_ref, state_ref)
            absorb(blocks, q_ref, m_ref, accl_ref)

    take(ok["u"](3), u3, u3s)
    take(ok["d"](3), d3, d3s)
    state = state_ref[...]
    high = state.astype(jnp.bfloat16)
    low = (state - high.astype(jnp.float32)).astype(jnp.bfloat16)
    for h in range(8):
        qf = qf_ref[h]
        nd = stu_ref[h] + nn(qf, high) + nn(qf, low)
        student = nd[:, 0:HD] / (nd[:, HD:] + epsilon)
        accl = accl_ref[h]
        teacher = (accl[:, 0:HD] / accl[:, HD:]).astype(jnp.bfloat16).astype(jnp.float32)
        out_ref[:, h * HD : (h + 1) * HD] = (2.0 * (student - teacher)).astype(jnp.bfloat16)


def per_device(queries, keys, values, query_map, key_map, positions):
    f32, bf16 = jnp.float32, jnp.bfloat16
    any_ = pl.BlockSpec(memory_space=pl.ANY)
    vm = pl.BlockSpec(memory_space=pltpu.VMEM)
    own = pl.pallas_call(
        pack_kernel,
        out_shape=jax.ShapeDtypeStruct((ROWS, 2 * HD), bf16),
        in_specs=[any_, any_, vm],
        out_specs=vm,
        scratch_shapes=[pltpu.SemaphoreType.DMA((2,))],
        name="pack",
    )(keys, values, positions.reshape(1, TOK))
    swap = lambda a: lax.ppermute(a, "c", SWAP)
    u1 = lax.ppermute(own, "z", ring(1))
    d1 = lax.ppermute(own, "z", ring(-1))
    x4 = lax.ppermute(own, "z", ring(4))
    u2 = lax.ppermute(u1, "z", ring(1))
    d2 = lax.ppermute(d1, "z", ring(-1))
    u3 = lax.ppermute(u2, "z", ring(1))
    d3 = lax.ppermute(d2, "z", ring(-1))

    heads = lambda w, t: jax.ShapeDtypeStruct((8, TOK, w), t)
    state = jax.ShapeDtypeStruct((2 * HD, 2 * HD), f32)
    qf, m, accl, stu = call(
        local_kernel,
        (heads(256, bf16), heads(HD, f32), heads(256, f32), heads(256, f32)),
        flops=8 * 2 * 256 * 128 * 1500,
        nbytes=8 << 20,
        name="own",
    )(own, queries, query_map, key_map)
    arrivals = [swap(own)]
    for a in (u1, d1, x4, u2, d2):
        arrivals += [a, swap(a)]
    m, accl, st = call(
        mid_kernel,
        (heads(HD, f32), heads(256, f32), state),
        flops=8 * 2 * 256 * 128 * 6000,
        nbytes=8 << 20,
        name="mid",
    )(*arrivals, queries, key_map, m, accl)
    tail = [u3, swap(u3), d3, swap(d3)]
    return call(
        last_kernel,
        jax.ShapeDtypeStruct((TOK, 8 * HD), bf16),
        scratch=(
            pltpu.VMEM((8, TOK, HD), f32),
            pltpu.VMEM((8, TOK, 256), f32),
            pltpu.VMEM((2 * HD, 2 * HD), f32),
        ),
        flops=8 * 2 * 256 * 128 * 3000,
        nbytes=8 << 20,
        name="last",
    )(*tail, queries, key_map, qf, stu, m, accl, st)


def solution(mesh):
    split = Mesh(mesh.devices.reshape(8, 2, mesh.shape["head"]), ("z", "c", "head"))
    seq = ("z", "c")
    placed = (P(seq, "head"), P(seq, None), P(seq, None), P("head", None, None), P(), P(seq))
    return jax.shard_map(
        per_device, mesh=split, in_specs=placed, out_specs=P(seq, "head"), check_vma=False
    )
```

```python
import math

import jax
import jax.numpy as jnp
from jax import lax
from jax.experimental import pallas as pl
from jax.experimental.pallas import tpu as pltpu
from jax.sharding import Mesh
from jax.sharding import PartitionSpec as P


QHEADS = 128
KVH = 8
LENGTH = 131072
HD = 128
ROWS = 272
TOK = 256
epsilon = 1e-06
masked_score = -1e30
to_exp2 = math.log2(math.e) / math.sqrt(HD)

SWAP = [(0, 1), (1, 0)]


def ring(shift):
    return [(i, (i + shift) % 8) for i in range(8)]


def call(kernel, out_shape, in_specs=None, scratch=(), flops=0, nbytes=0, transcendentals=0):
    more = {} if in_specs is None else {"in_specs": in_specs}
    return pl.pallas_call(
        kernel,
        out_shape=out_shape,
        **more,
        scratch_shapes=list(scratch),
        compiler_params=pltpu.CompilerParams(vmem_limit_bytes=40 * 1024 * 1024),
        cost_estimate=pl.CostEstimate(
            flops=flops, bytes_accessed=nbytes, transcendentals=transcendentals
        ),
    )


def first_group(local_heads):
    return lax.axis_index("head") * local_heads // (QHEADS // KVH)


def pieces(x):
    a = x.astype(jnp.bfloat16)
    x = x - a.astype(jnp.float32)
    b = x.astype(jnp.bfloat16)
    c = (x - b.astype(jnp.float32)).astype(jnp.bfloat16)
    return a.astype(jnp.float32), b.astype(jnp.float32), c.astype(jnp.float32)


def pack_kernel(keys_ref, values_ref, pos_ref, out_ref, pos_vmem, sems):
    g = pl.multiple_of(first_group(8) * HD, HD)
    cp = pltpu.make_async_copy(pos_ref, pos_vmem, sems.at[2])
    ck = pltpu.make_async_copy(keys_ref.at[:, pl.ds(g, HD)], out_ref.at[0:TOK, 0:HD], sems.at[0])
    cv = pltpu.make_async_copy(
        values_ref.at[:, pl.ds(g, HD)], out_ref.at[0:TOK, HD : 2 * HD], sems.at[1]
    )
    cp.start()
    ck.start()
    cv.start()
    cp.wait()
    a = (0.5 * math.pi / LENGTH) * pos_vmem[...].astype(jnp.float32)
    row = lax.broadcasted_iota(jnp.int32, (16, TOK), 0)
    tile = jnp.zeros((16, TOK), jnp.float32)
    for i, part in enumerate(pieces(jnp.cos(a)) + pieces(jnp.sin(a))):
        tile = jnp.where(row == i, part, tile)
    out_ref[TOK:ROWS, :] = tile.astype(jnp.bfloat16)
    ck.wait()
    cv.wait()


def angles_of(block_ref):
    d = block_ref[TOK:ROWS, :].astype(jnp.float32)
    return d[0:1] + d[1:2] + d[2:3], d[3:4] + d[4:5] + d[5:6]


def elu1(x):
    return jnp.where(x > 0.0, x + 1.0, jnp.exp(jnp.minimum(x, 0.0)))


def dot(a, b, dims):
    return lax.dot_general(a, b, (dims, ((), ())), preferred_element_type=jnp.float32)


def nn(a, b):
    return dot(a, b, ((1,), (0,)))


def nt(a, b):
    return dot(a, b, ((1,), (1,)))


def key_feats_t(block_ref, key_map, ok=None):
    c, s = angles_of(block_ref)
    if ok is not None:
        c, s = jnp.where(ok, c, 0.0), jnp.where(ok, s, 0.0)
    phi = elu1(dot(key_map, block_ref[0:TOK, 0:HD], ((0,), (1,))))
    return jnp.concatenate([c * phi, s * phi], axis=0).astype(jnp.bfloat16)


def with_ones(v):
    return jnp.concatenate([v, jnp.ones(v.shape, v.dtype)], axis=1)


def local_kernel(own_ref, q_ref, qmap_ref, kmap_ref, qf_ref, m_ref, accl_ref, stu_ref):
    k = own_ref[0:TOK, 0:HD]
    va = with_ones(own_ref[0:TOK, HD : 2 * HD])
    c, s = angles_of(own_ref)
    ct = jnp.broadcast_to(c, (HD, TOK)).T
    st = jnp.broadcast_to(s, (HD, TOK)).T
    kft = key_feats_t(own_ref, kmap_ref[first_group(8)])
    causal = lax.broadcasted_iota(jnp.int32, (TOK, TOK), 0) >= lax.broadcasted_iota(
        jnp.int32, (TOK, TOK), 1
    )
    for h in range(8):
        q = q_ref[:, h * HD : (h + 1) * HD]
        phi = elu1(nn(q, qmap_ref[h]))
        qf = jnp.concatenate([ct * phi, st * phi], axis=1).astype(jnp.bfloat16)
        qf_ref[h] = qf
        inner = jnp.where(causal, nn(qf, kft), 0.0).astype(jnp.bfloat16)
        stu_ref[h] = nn(inner, va)
        x = jnp.where(causal, nt(q, k), masked_score)
        m = jnp.max(x, axis=1, keepdims=True)
        p = jnp.exp2((x - m) * to_exp2).astype(jnp.bfloat16)
        accl_ref[h] = nn(p, va)
        m_ref[h] = jnp.broadcast_to(m, (TOK, HD))


def absorb(blocks, q_ref, kmap_ref, m_ref, accl_ref, state_ref):
    km = kmap_ref[first_group(8)]
    va = jnp.concatenate([with_ones(b[0:TOK, HD : 2 * HD]) for b, _ in blocks], axis=0)
    feats = [None] * len(blocks)
    for h in range(8):
        q = q_ref[:, h * HD : (h + 1) * HD]
        xs = [nt(q, b[0:TOK, 0:HD]) for b, _ in blocks]
        for i in range(h, len(blocks), 8):
            feats[i] = key_feats_t(blocks[i][0], km, blocks[i][1])
        m0 = m_ref[h]
        top = None
        for x, (_, ok) in zip(xs, blocks):
            t = jnp.where(ok, jnp.maximum(x[:, 0:HD], x[:, HD:]), masked_score)
            top = t if top is None else jnp.maximum(top, t)
        top = jnp.max(top, axis=1, keepdims=True)
        m1 = jnp.maximum(m0, jnp.broadcast_to(top, m0.shape))
        f = jnp.exp2((m0 - m1) * to_exp2)
        ps = []
        for x, (_, ok) in zip(xs, blocks):
            mm = jnp.where(ok, m1, -masked_score)
            p = jnp.exp2((x - jnp.concatenate([mm, mm], axis=1)) * to_exp2)
            ps.append(p.astype(jnp.bfloat16))
        add = nn(jnp.concatenate(ps, axis=1), va)
        accl_ref[h] = accl_ref[h] * jnp.concatenate([f, f], axis=1) + add
        m_ref[h] = m1
    state_ref[...] += nn(jnp.concatenate(feats, axis=1), va)


def mid_kernel(pb, u1, u1s, d1, d1s, x, xs, u2, u2s, d2, d2s, q_ref, kmap_ref, m_in, accl_in,
               m_ref, accl_ref, state_ref):
    m_ref[...] = m_in[...]
    accl_ref[...] = accl_in[...]
    state_ref[...] = jnp.zeros_like(state_ref)
    z = lax.axis_index("z")
    rest = (q_ref, kmap_ref, m_ref, accl_ref, state_ref)
    second = lax.axis_index("c") == 1
    absorb(
        [(pb, second), (u1, z >= 1), (u1s, z >= 1), (x, z >= 4), (xs, z >= 4), (u2, z >= 2),
         (u2s, z >= 2)],
        *rest,
    )

    @pl.when(z >= 6)
    def _():
        absorb([(d1, z >= 7), (d1s, z >= 7), (d2, z >= 6), (d2s, z >= 6)], *rest)


def last_kernel(u3, u3s, d3, d3s, q_ref, kmap_ref, qf_ref, stu_ref, m_in, accl_in, state_in,
                out_ref, m_ref, accl_ref, state_ref):
    m_ref[...] = m_in[...]
    accl_ref[...] = accl_in[...]
    state_ref[...] = state_in[...]
    z = lax.axis_index("z")
    rest = (q_ref, kmap_ref, m_ref, accl_ref, state_ref)

    @pl.when(z >= 5)
    def _():
        absorb([(u3, z >= 3), (u3s, z >= 3), (d3, z >= 5), (d3s, z >= 5)], *rest)

    @pl.when((z >= 3) & (z < 5))
    def _():
        absorb([(u3, z >= 3), (u3s, z >= 3)], *rest)

    state = state_ref[...]
    high = state.astype(jnp.bfloat16)
    low = (state - high.astype(jnp.float32)).astype(jnp.bfloat16)
    for h in range(8):
        qf = qf_ref[h]
        nd = stu_ref[h] + nn(qf, high) + nn(qf, low)
        student = nd[:, 0:HD] / (nd[:, HD:] + epsilon)
        accl = accl_ref[h]
        teacher = (accl[:, 0:HD] / accl[:, HD:]).astype(jnp.bfloat16).astype(jnp.float32)
        out_ref[:, h * HD : (h + 1) * HD] = (2.0 * (student - teacher)).astype(jnp.bfloat16)


def per_device(queries, keys, values, query_map, key_map, positions):
    f32, bf16 = jnp.float32, jnp.bfloat16
    any_ = pl.BlockSpec(memory_space=pltpu.HBM)
    vm = pl.BlockSpec(memory_space=pltpu.VMEM)
    own = pl.pallas_call(
        pack_kernel,
        out_shape=jax.ShapeDtypeStruct((ROWS, 2 * HD), bf16),
        in_specs=[any_, any_, any_],
        out_specs=vm,
        scratch_shapes=[pltpu.VMEM((1, TOK), jnp.int32), pltpu.SemaphoreType.DMA((3,))],
        name="pack",
        cost_estimate=pl.CostEstimate(flops=4 << 30, bytes_accessed=16 << 20, transcendentals=0),
    )(keys, values, positions.reshape(1, TOK))
    swap = lambda a: lax.ppermute(a, "c", SWAP)

    def hop(a, shift):
        return lax.ppermute(a, "z", ring(shift))

    u1 = hop(own, 1)
    d1 = hop(own, -1)
    x4 = hop(own, 4)
    u2 = hop(u1, 1)
    d2 = hop(d1, -1)
    u3 = hop(u2, 1)
    d3 = hop(d2, -1)

    heads = lambda w, t: jax.ShapeDtypeStruct((8, TOK, w), t)
    state = jax.ShapeDtypeStruct((2 * HD, 2 * HD), f32)
    qf, m, accl, stu = call(
        local_kernel,
        (
            heads(256, bf16),
            heads(HD, f32),
            heads(256, f32),
            heads(256, f32),
        ),
        flops=8 * 2 * 256 * 128 * 1500,
        nbytes=8 << 20,
    )(own, queries, query_map, key_map)
    arrivals = [swap(own)]
    for a in (u1, d1, x4, u2, d2):
        arrivals += [a, swap(a)]
    m, accl, st = call(
        mid_kernel,
        (heads(HD, f32), heads(256, f32), state),
        flops=8 * 2 * 256 * 128 * 6000,
        nbytes=8 << 20,
    )(*arrivals, queries, key_map, m, accl)
    tail = [u3, swap(u3), d3, swap(d3)]
    return call(
        last_kernel,
        jax.ShapeDtypeStruct((TOK, 8 * HD), bf16),
        scratch=(
            pltpu.VMEM((8, TOK, HD), f32),
            pltpu.VMEM((8, TOK, 256), f32),
            pltpu.VMEM((2 * HD, 2 * HD), f32),
        ),
        flops=8 * 2 * 256 * 128 * 3000,
        nbytes=8 << 20,
    )(*tail, queries, key_map, qf, stu, m, accl, st)


def solution(mesh):
    split = Mesh(mesh.devices.reshape(8, 2, mesh.shape["head"]), ("z", "c", "head"))
    seq = ("z", "c")
    placed = (P(seq, "head"), P(seq, None), P(seq, None), P("head", None, None), P(), P(seq))
    return jax.shard_map(
        per_device, mesh=split, in_specs=placed, out_specs=P(seq, "head"), check_vma=False
    )
```

```python
import math

import jax
import jax.numpy as jnp
from jax import lax
from jax.experimental import pallas as pl
from jax.experimental.pallas import tpu as pltpu
from jax.sharding import Mesh
from jax.sharding import PartitionSpec as P


QHEADS = 128
KVH = 8
LENGTH = 131072
HD = 128
ROWS = 272
TOK = 256
epsilon = 1e-06
masked_score = -1e30
to_exp2 = math.log2(math.e) / math.sqrt(HD)

SWAP = [(0, 1), (1, 0)]


def ring(shift):
    return [(i, (i + shift) % 8) for i in range(8)]


def call(kernel, out_shape, in_specs=None, scratch=(), flops=0, nbytes=0,
         aliases=None):
    more = {} if in_specs is None else {"in_specs": in_specs}
    return pl.pallas_call(
        kernel,
        out_shape=out_shape,
        **more,
        input_output_aliases=aliases or {},
        scratch_shapes=list(scratch),
        compiler_params=pltpu.CompilerParams(vmem_limit_bytes=40 * 1024 * 1024),
        cost_estimate=pl.CostEstimate(
            flops=flops, bytes_accessed=nbytes, transcendentals=0
        ),
    )


def first_group(local_heads):
    return lax.axis_index("head") * local_heads // (QHEADS // KVH)


def pieces(x):
    a = x.astype(jnp.bfloat16)
    x = x - a.astype(jnp.float32)
    b = x.astype(jnp.bfloat16)
    c = (x - b.astype(jnp.float32)).astype(jnp.bfloat16)
    return a.astype(jnp.float32), b.astype(jnp.float32), c.astype(jnp.float32)


def pack_kernel(keys_ref, values_ref, pos_ref, out_ref, pos_vmem, sems):
    g = pl.multiple_of(first_group(8) * HD, HD)
    cp = pltpu.make_async_copy(pos_ref, pos_vmem, sems.at[2])
    ck = pltpu.make_async_copy(keys_ref.at[:, pl.ds(g, HD)], out_ref.at[0:TOK, 0:HD], sems.at[0])
    cv = pltpu.make_async_copy(
        values_ref.at[:, pl.ds(g, HD)], out_ref.at[0:TOK, HD : 2 * HD], sems.at[1]
    )
    cp.start()
    ck.start()
    cv.start()
    cp.wait()
    a = (0.5 * math.pi / LENGTH) * pos_vmem[...].astype(jnp.float32)
    row = lax.broadcasted_iota(jnp.int32, (16, TOK), 0)
    tile = jnp.zeros((16, TOK), jnp.float32)
    for i, part in enumerate(pieces(jnp.cos(a)) + pieces(jnp.sin(a))):
        tile = jnp.where(row == i, part, tile)
    out_ref[TOK:ROWS, :] = tile.astype(jnp.bfloat16)
    ck.wait()
    cv.wait()


def angles_of(block_ref):
    d = block_ref[TOK:ROWS, :].astype(jnp.float32)
    return d[0:1] + d[1:2] + d[2:3], d[3:4] + d[4:5] + d[5:6]


def elu1(x):
    return jnp.where(x > 0.0, x + 1.0, jnp.exp(jnp.minimum(x, 0.0)))


def dot(a, b, dims):
    return lax.dot_general(a, b, (dims, ((), ())), preferred_element_type=jnp.float32)


def nn(a, b):
    return dot(a, b, ((1,), (0,)))


def nt(a, b):
    return dot(a, b, ((1,), (1,)))


def key_feats_t(block_ref, key_map, ok=None):
    c, s = angles_of(block_ref)
    if ok is not None:
        c, s = jnp.where(ok, c, 0.0), jnp.where(ok, s, 0.0)
    phi = elu1(dot(key_map, block_ref[0:TOK, 0:HD], ((0,), (1,))))
    return jnp.concatenate([c * phi, s * phi], axis=0).astype(jnp.bfloat16)


def with_ones(v):
    return jnp.concatenate([v, jnp.ones(v.shape, v.dtype)], axis=1)


def local_kernel(own_ref, q_ref, qmap_ref, kmap_ref, qf_ref, m_ref, accl_ref, stu_ref):
    k = own_ref[0:TOK, 0:HD]
    va = with_ones(own_ref[0:TOK, HD : 2 * HD])
    c, s = angles_of(own_ref)
    ct = jnp.broadcast_to(c, (HD, TOK)).T
    st = jnp.broadcast_to(s, (HD, TOK)).T
    kft = key_feats_t(own_ref, kmap_ref[first_group(8)])
    causal = lax.broadcasted_iota(jnp.int32, (TOK, TOK), 0) >= lax.broadcasted_iota(
        jnp.int32, (TOK, TOK), 1
    )
    for h in range(8):
        q = q_ref[:, h * HD : (h + 1) * HD]
        phi = elu1(nn(q, qmap_ref[h]))
        qf = jnp.concatenate([ct * phi, st * phi], axis=1).astype(jnp.bfloat16)
        qf_ref[h] = qf
        inner = jnp.where(causal, nn(qf, kft), 0.0).astype(jnp.bfloat16)
        stu_ref[h] = nn(inner, va)
        x = jnp.where(causal, nt(q, k), masked_score)
        m = jnp.max(x, axis=1, keepdims=True)
        p = jnp.exp2((x - m) * to_exp2).astype(jnp.bfloat16)
        accl_ref[h] = nn(p, va)
        m_ref[h] = jnp.broadcast_to(m, (TOK, HD))


def scores_of(q_ref, h, blocks):
    q = q_ref[:, h * HD : (h + 1) * HD]
    return [nt(q, b[0:TOK, 0:HD]) for b, _ in blocks]


def softmax_step(xs, blocks, va, m0, accl):
    top = None
    for x, (_, ok) in zip(xs, blocks):
        t = jnp.where(ok, jnp.maximum(x[:, 0:HD], x[:, HD:]), masked_score)
        top = t if top is None else jnp.maximum(top, t)
    top = jnp.max(top, axis=1, keepdims=True)
    m1 = jnp.maximum(m0, jnp.broadcast_to(top, m0.shape))
    f = jnp.exp2((m0 - m1) * to_exp2)
    ps = []
    for x, (_, ok) in zip(xs, blocks):
        mm = jnp.where(ok, m1, -masked_score)
        p = jnp.exp2((x - jnp.concatenate([mm, mm], axis=1)) * to_exp2)
        ps.append(p.astype(jnp.bfloat16))
    add = nn(jnp.concatenate(ps, axis=1), va)
    return m1, accl * jnp.concatenate([f, f], axis=1) + add


def values_of(blocks):
    return jnp.concatenate([with_ones(b[0:TOK, HD : 2 * HD]) for b, _ in blocks], axis=0)


def absorb(blocks, q_ref, kmap_ref, m_from, accl_from, state, m_ref, accl_ref):
    km = kmap_ref[first_group(8)]
    va = values_of(blocks)
    feats = [None] * len(blocks)
    later = scores_of(q_ref, 0, blocks)
    for h in range(8):
        xs = later
        if h < 7:
            later = scores_of(q_ref, h + 1, blocks)
        for i in range(h, len(blocks), 8):
            feats[i] = key_feats_t(blocks[i][0], km, blocks[i][1])
        m_ref[h], accl_ref[h] = softmax_step(xs, blocks, va, m_from[h], accl_from[h])
    return state + nn(jnp.concatenate(feats, axis=1), va)


def near_kernel(pb, u1, u1s, d1, d1s, q_ref, kmap_ref, m_in, accl_in, m_ref, accl_ref, state_ref):
    z = lax.axis_index("z")
    second = lax.axis_index("c") == 1
    ins = (q_ref, kmap_ref, m_in, accl_in)
    outs = (m_ref, accl_ref)

    @pl.when(z == 0)
    def _():
        state_ref[...] = absorb([(pb, second)], *ins, 0.0, *outs)

    @pl.when(z >= 1)
    def _():
        blocks = [(pb, second), (u1, z >= 1), (u1s, z >= 1)]
        state_ref[...] = absorb(blocks, *ins, 0.0, *outs)

    @pl.when(z >= 7)
    def _():
        blocks = [(d1, z >= 7), (d1s, z >= 7)]
        state_ref[...] = absorb(blocks, q_ref, kmap_ref, m_ref, accl_ref, state_ref[...], *outs)


def mid_kernel(x, xs, u2, u2s, d2, d2s, q_ref, kmap_ref, m_in, accl_in, state_in,
               m_ref, accl_ref, state_ref):
    z = lax.axis_index("z")
    blocks = [(u2, z >= 2), (u2s, z >= 2), (x, z >= 4), (xs, z >= 4)]

    @pl.when((z >= 2) & (z < 6))
    def _():
        state_ref[...] = absorb(
            blocks, q_ref, kmap_ref, m_in, accl_in, state_in[...], m_ref, accl_ref
        )

    @pl.when(z >= 6)
    def _():
        state_ref[...] = absorb(
            blocks + [(d2, z >= 6), (d2s, z >= 6)],
            q_ref, kmap_ref, m_in, accl_in, state_in[...], m_ref, accl_ref,
        )


def edge_kernel(u3, d3, q_ref, kmap_ref, m_in, accl_in, state_in, m_ref, accl_ref, state_ref):
    z = lax.axis_index("z")
    ins = (q_ref, kmap_ref, m_in, accl_in)

    @pl.when((z >= 3) & (z < 5))
    def _():
        state_ref[...] = absorb([(u3, z >= 3)], *ins, state_in[...], m_ref, accl_ref)

    @pl.when(z >= 5)
    def _():
        blocks = [(u3, z >= 3), (d3, z >= 5)]
        state_ref[...] = absorb(blocks, *ins, state_in[...], m_ref, accl_ref)


def last_kernel(u3s, d3s, q_ref, kmap_ref, qf_ref, stu_ref, m_in, accl_in, state_in,
                out_ref):
    z = lax.axis_index("z")

    def finish(blocks):
        state = state_in[...]
        if blocks:
            km = kmap_ref[first_group(8)]
            va = values_of(blocks)
            feats = [key_feats_t(b, km, ok) for b, ok in blocks]
            later = scores_of(q_ref, 0, blocks)
            state = state + nn(jnp.concatenate(feats, axis=1), va)
        high = state.astype(jnp.bfloat16)
        for h in range(8):
            accl = accl_in[h]
            if blocks:
                xs = later
                if h < 7:
                    later = scores_of(q_ref, h + 1, blocks)
                _, accl = softmax_step(xs, blocks, va, m_in[h], accl)
            qf = qf_ref[h]
            nd = stu_ref[h] + nn(qf, high)
            student = nd[:, 0:HD] / (nd[:, HD:] + epsilon)
            teacher = (accl[:, 0:HD] / accl[:, HD:]).astype(jnp.bfloat16).astype(jnp.float32)
            out_ref[:, h * HD : (h + 1) * HD] = (2.0 * (student - teacher)).astype(jnp.bfloat16)

    near = [(u3s, z >= 3)]

    @pl.when(z >= 5)
    def _():
        finish(near + [(d3s, z >= 5)])

    @pl.when((z >= 3) & (z < 5))
    def _():
        finish(near)

    @pl.when(z < 3)
    def _():
        finish([])


def per_device(queries, keys, values, query_map, key_map, positions):
    f32, bf16 = jnp.float32, jnp.bfloat16
    any_ = pl.BlockSpec(memory_space=pltpu.HBM)
    vm = pl.BlockSpec(memory_space=pltpu.VMEM)
    own = pl.pallas_call(
        pack_kernel,
        out_shape=jax.ShapeDtypeStruct((ROWS, 2 * HD), bf16),
        in_specs=[any_, any_, any_],
        out_specs=vm,
        scratch_shapes=[pltpu.VMEM((1, TOK), jnp.int32), pltpu.SemaphoreType.DMA((3,))],
        name="pack",
        cost_estimate=pl.CostEstimate(flops=4 << 30, bytes_accessed=16 << 20, transcendentals=0),
    )(keys, values, positions.reshape(1, TOK))

    def swap(a):
        return lax.ppermute(a, "c", SWAP)

    def hop(a, shift):
        return lax.ppermute(a, "z", ring(shift))

    u1 = hop(own, 1)
    d1 = hop(own, -1)
    x4 = hop(own, 4)
    u2 = hop(u1, 1)
    d2 = hop(d1, -1)
    u3 = hop(u2, 1)
    d3 = hop(d2, -1)

    heads = lambda w, t: jax.ShapeDtypeStruct((8, TOK, w), t)
    state = jax.ShapeDtypeStruct((2 * HD, 2 * HD), f32)
    qf, m, accl, stu = call(
        local_kernel,
        (
            heads(256, bf16),
            heads(HD, f32),
            heads(256, f32),
            heads(256, f32),
        ),
        flops=8 * 2 * 256 * 128 * 1500,
        nbytes=8 << 20,
    )(own, queries, query_map, key_map)
    m, accl, st = call(
        near_kernel,
        (heads(HD, f32), heads(256, f32), state),
        flops=8 * 2 * 256 * 128 * 3000,
        nbytes=8 << 20,
        aliases={7: 0, 8: 1},
    )(swap(own), u1, swap(u1), d1, swap(d1), queries, key_map, m, accl)
    m, accl, st = call(
        mid_kernel,
        (heads(HD, f32), heads(256, f32), state),
        flops=8 * 2 * 256 * 128 * 4000,
        nbytes=8 << 20,
        aliases={8: 0, 9: 1, 10: 2},
    )(x4, swap(x4), u2, swap(u2), d2, swap(d2), queries, key_map, m,
      accl, st)
    m, accl, st = call(
        edge_kernel,
        (heads(HD, f32), heads(256, f32), state),
        flops=8 * 2 * 256 * 128 * 1500,
        nbytes=8 << 20,
        aliases={4: 0, 5: 1, 6: 2},
    )(u3, d3, queries, key_map, m, accl, st)
    return call(
        last_kernel,
        jax.ShapeDtypeStruct((TOK, 8 * HD), bf16),
        flops=8 * 2 * 256 * 128 * 3000,
        nbytes=8 << 20,
    )(swap(u3), swap(d3), queries, key_map, qf, stu, m, accl, st)


def solution(mesh):
    split = Mesh(mesh.devices.reshape(8, 2, mesh.shape["head"]), ("z", "c", "head"))
    seq = ("z", "c")
    placed = (P(seq, "head"), P(seq, None), P(seq, None), P("head", None, None), P(), P(seq))
    return jax.shard_map(
        per_device, mesh=split, in_specs=placed, out_specs=P(seq, "head"), check_vma=False
    )
```

```python
import math

import jax
import jax.numpy as jnp
from jax import lax
from jax.experimental import pallas as pl
from jax.experimental.pallas import tpu as pltpu
from jax.sharding import Mesh
from jax.sharding import PartitionSpec as P


QHEADS = 128
KVH = 8
LENGTH = 131072
HD = 128
ROWS = 272
TOK = 256
epsilon = 1e-06
masked_score = -1e30
to_exp2 = math.log2(math.e) / math.sqrt(HD)

SWAP = [(0, 1), (1, 0)]


def ring(shift):
    return [(i, (i + shift) % 8) for i in range(8)]


def call(kernel, out_shape, in_specs=None, scratch=(), flops=0, nbytes=0,
         aliases=None):
    more = {} if in_specs is None else {"in_specs": in_specs}
    return pl.pallas_call(
        kernel,
        out_shape=out_shape,
        **more,
        input_output_aliases=aliases or {},
        scratch_shapes=list(scratch),
        compiler_params=pltpu.CompilerParams(vmem_limit_bytes=40 * 1024 * 1024),
        cost_estimate=pl.CostEstimate(
            flops=flops, bytes_accessed=nbytes, transcendentals=0
        ),
    )


def first_group(local_heads):
    return lax.axis_index("head") * local_heads // (QHEADS // KVH)


def pieces(x):
    a = x.astype(jnp.bfloat16)
    x = x - a.astype(jnp.float32)
    b = x.astype(jnp.bfloat16)
    c = (x - b.astype(jnp.float32)).astype(jnp.bfloat16)
    return a.astype(jnp.float32), b.astype(jnp.float32), c.astype(jnp.float32)


def pack_kernel(keys_ref, values_ref, pos_ref, out_ref, pos_vmem, sems):
    g = pl.multiple_of(first_group(8) * HD, HD)
    cp = pltpu.make_async_copy(pos_ref, pos_vmem, sems.at[2])
    ck = pltpu.make_async_copy(keys_ref.at[:, pl.ds(g, HD)], out_ref.at[0:TOK, 0:HD], sems.at[0])
    cv = pltpu.make_async_copy(
        values_ref.at[:, pl.ds(g, HD)], out_ref.at[0:TOK, HD : 2 * HD], sems.at[1]
    )
    cp.start()
    ck.start()
    cv.start()
    cp.wait()
    a = (0.5 * math.pi / LENGTH) * pos_vmem[...].astype(jnp.float32)
    row = lax.broadcasted_iota(jnp.int32, (16, TOK), 0)
    tile = jnp.zeros((16, TOK), jnp.float32)
    for i, part in enumerate(pieces(jnp.cos(a)) + pieces(jnp.sin(a))):
        tile = jnp.where(row == i, part, tile)
    out_ref[TOK:ROWS, :] = tile.astype(jnp.bfloat16)
    ck.wait()
    cv.wait()


def angles_of(block_ref):
    d = block_ref[TOK:ROWS, :].astype(jnp.float32)
    return d[0:1] + d[1:2] + d[2:3], d[3:4] + d[4:5] + d[5:6]


def elu1(x):
    return jnp.where(x > 0.0, x + 1.0, jnp.exp(jnp.minimum(x, 0.0)))


def dot(a, b, dims):
    return lax.dot_general(a, b, (dims, ((), ())), preferred_element_type=jnp.float32)


def nn(a, b):
    return dot(a, b, ((1,), (0,)))


def nt(a, b):
    return dot(a, b, ((1,), (1,)))


def key_feats_t(block_ref, key_map, ok=None):
    c, s = angles_of(block_ref)
    if ok is not None:
        c, s = jnp.where(ok, c, 0.0), jnp.where(ok, s, 0.0)
    phi = elu1(dot(key_map, block_ref[0:TOK, 0:HD], ((0,), (1,))))
    return jnp.concatenate([c * phi, s * phi], axis=0).astype(jnp.bfloat16)


def with_ones(v):
    return jnp.concatenate([v, jnp.ones(v.shape, v.dtype)], axis=1)


def local_kernel(own_ref, q_ref, qmap_ref, kmap_ref, qf_ref, m_ref, accl_ref, stu_ref):
    k = own_ref[0:TOK, 0:HD]
    va = with_ones(own_ref[0:TOK, HD : 2 * HD])
    c, s = angles_of(own_ref)
    ct = jnp.broadcast_to(c, (HD, TOK)).T
    st = jnp.broadcast_to(s, (HD, TOK)).T
    kft = key_feats_t(own_ref, kmap_ref[first_group(8)])
    causal = lax.broadcasted_iota(jnp.int32, (TOK, TOK), 0) >= lax.broadcasted_iota(
        jnp.int32, (TOK, TOK), 1
    )
    for h in range(8):
        q = q_ref[:, h * HD : (h + 1) * HD]
        phi = elu1(nn(q, qmap_ref[h]))
        qf = jnp.concatenate([ct * phi, st * phi], axis=1).astype(jnp.bfloat16)
        qf_ref[h] = qf
        inner = jnp.where(causal, nn(qf, kft), 0.0).astype(jnp.bfloat16)
        stu_ref[h] = nn(inner, va)
        x = jnp.where(causal, nt(q, k), masked_score)
        m = jnp.max(x, axis=1, keepdims=True)
        p = jnp.exp2((x - m) * to_exp2).astype(jnp.bfloat16)
        accl_ref[h] = nn(p, va)
        m_ref[h] = jnp.broadcast_to(m, (TOK, HD))


def scores_of(q_ref, h, blocks):
    q = q_ref[:, h * HD : (h + 1) * HD]
    return [nt(q, b[0:TOK, 0:HD]) for b, _ in blocks]


def softmax_step(xs, blocks, va, m0, accl):
    top = None
    for x, (_, ok) in zip(xs, blocks):
        t = jnp.where(ok, jnp.maximum(x[:, 0:HD], x[:, HD:]), masked_score)
        top = t if top is None else jnp.maximum(top, t)
    top = jnp.max(top, axis=1, keepdims=True)
    m1 = jnp.maximum(m0, jnp.broadcast_to(top, m0.shape))
    f = jnp.exp2((m0 - m1) * to_exp2)
    ps = []
    for x, (_, ok) in zip(xs, blocks):
        mm = jnp.where(ok, m1, -masked_score)
        p = jnp.exp2((x - jnp.concatenate([mm, mm], axis=1)) * to_exp2)
        ps.append(p.astype(jnp.bfloat16))
    add = nn(jnp.concatenate(ps, axis=1), va)
    return m1, accl * jnp.concatenate([f, f], axis=1) + add


def values_of(blocks):
    return jnp.concatenate([with_ones(b[0:TOK, HD : 2 * HD]) for b, _ in blocks], axis=0)


def absorb(blocks, q_ref, kmap_ref, m_from, accl_from, state, m_ref, accl_ref):
    km = kmap_ref[first_group(8)]
    va = values_of(blocks)
    feats = [None] * len(blocks)
    later = scores_of(q_ref, 0, blocks)
    for h in range(8):
        xs = later
        if h < 7:
            later = scores_of(q_ref, h + 1, blocks)
        for i in range(h, len(blocks), 8):
            feats[i] = key_feats_t(blocks[i][0], km, blocks[i][1])
        m_ref[h], accl_ref[h] = softmax_step(xs, blocks, va, m_from[h], accl_from[h])
    return state + nn(jnp.concatenate(feats, axis=1), va)


def near_kernel(pb, u1, u1s, q_ref, kmap_ref, m_in, accl_in, m_ref, accl_ref, state_ref):
    z = lax.axis_index("z")
    second = lax.axis_index("c") == 1
    ins = (q_ref, kmap_ref, m_in, accl_in)
    outs = (m_ref, accl_ref)

    @pl.when(z == 0)
    def _():
        state_ref[...] = absorb([(pb, second)], *ins, 0.0, *outs)

    @pl.when(z >= 1)
    def _():
        blocks = [(pb, second), (u1, z >= 1), (u1s, z >= 1)]
        state_ref[...] = absorb(blocks, *ins, 0.0, *outs)


def wrap_kernel(d1, d1s, q_ref, kmap_ref, m_in, accl_in, state_in, m_ref, accl_ref, state_ref):
    z = lax.axis_index("z")

    @pl.when(z >= 7)
    def _():
        blocks = [(d1, z >= 7), (d1s, z >= 7)]
        state_ref[...] = absorb(
            blocks, q_ref, kmap_ref, m_in, accl_in, state_in[...], m_ref, accl_ref
        )


def mid_kernel(u2, u2s, d2, d2s, q_ref, kmap_ref, m_in, accl_in, state_in,
               m_ref, accl_ref, state_ref):
    z = lax.axis_index("z")
    blocks = [(u2, z >= 2), (u2s, z >= 2)]

    @pl.when((z >= 2) & (z < 6))
    def _():
        state_ref[...] = absorb(
            blocks, q_ref, kmap_ref, m_in, accl_in, state_in[...], m_ref, accl_ref
        )

    @pl.when(z >= 6)
    def _():
        state_ref[...] = absorb(
            blocks + [(d2, z >= 6), (d2s, z >= 6)],
            q_ref, kmap_ref, m_in, accl_in, state_in[...], m_ref, accl_ref,
        )


def far_kernel(x, xs, q_ref, kmap_ref, m_in, accl_in, state_in, m_ref, accl_ref, state_ref):
    z = lax.axis_index("z")

    @pl.when(z >= 4)
    def _():
        state_ref[...] = absorb(
            [(x, z >= 4), (xs, z >= 4)],
            q_ref, kmap_ref, m_in, accl_in, state_in[...], m_ref, accl_ref,
        )


def last_kernel(u3, u3s, d3, d3s, q_ref, kmap_ref, qf_ref, stu_ref, m_in, accl_in, state_in,
                out_ref):
    z = lax.axis_index("z")

    def finish(blocks):
        state = state_in[...]
        if blocks:
            km = kmap_ref[first_group(8)]
            va = values_of(blocks)
            feats = [key_feats_t(b, km, ok) for b, ok in blocks]
            later = scores_of(q_ref, 0, blocks)
            state = state + nn(jnp.concatenate(feats, axis=1), va)
        high = state.astype(jnp.bfloat16)
        for h in range(8):
            accl = accl_in[h]
            if blocks:
                xs = later
                if h < 7:
                    later = scores_of(q_ref, h + 1, blocks)
                _, accl = softmax_step(xs, blocks, va, m_in[h], accl)
            qf = qf_ref[h]
            nd = stu_ref[h] + nn(qf, high)
            student = nd[:, 0:HD] / (nd[:, HD:] + epsilon)
            teacher = (accl[:, 0:HD] / accl[:, HD:]).astype(jnp.bfloat16).astype(jnp.float32)
            out_ref[:, h * HD : (h + 1) * HD] = (2.0 * (student - teacher)).astype(jnp.bfloat16)

    near = [(u3, z >= 3), (u3s, z >= 3)]

    @pl.when(z >= 5)
    def _():
        finish(near + [(d3, z >= 5), (d3s, z >= 5)])

    @pl.when((z >= 3) & (z < 5))
    def _():
        finish(near)

    @pl.when(z < 3)
    def _():
        finish([])


def per_device(queries, keys, values, query_map, key_map, positions):
    f32, bf16 = jnp.float32, jnp.bfloat16
    any_ = pl.BlockSpec(memory_space=pltpu.HBM)
    vm = pl.BlockSpec(memory_space=pltpu.VMEM)
    own = pl.pallas_call(
        pack_kernel,
        out_shape=jax.ShapeDtypeStruct((ROWS, 2 * HD), bf16),
        in_specs=[any_, any_, any_],
        out_specs=vm,
        scratch_shapes=[pltpu.VMEM((1, TOK), jnp.int32), pltpu.SemaphoreType.DMA((3,))],
        name="pack",
        cost_estimate=pl.CostEstimate(flops=4 << 30, bytes_accessed=16 << 20, transcendentals=0),
    )(keys, values, positions.reshape(1, TOK))

    def swap(a):
        return lax.ppermute(a, "c", SWAP)

    def hop(a, shift):
        return lax.ppermute(a, "z", ring(shift))

    u1 = hop(own, 1)
    d1 = hop(own, -1)
    x4 = hop(own, 4)
    u2 = hop(u1, 1)
    d2 = hop(d1, -1)
    u3 = hop(u2, 1)
    d3 = hop(d2, -1)

    heads = lambda w, t: jax.ShapeDtypeStruct((8, TOK, w), t)
    state = jax.ShapeDtypeStruct((2 * HD, 2 * HD), f32)
    qf, m, accl, stu = call(
        local_kernel,
        (
            heads(256, bf16),
            heads(HD, f32),
            heads(256, f32),
            heads(256, f32),
        ),
        flops=8 * 2 * 256 * 128 * 1500,
        nbytes=8 << 20,
    )(own, queries, query_map, key_map)
    m, accl, st = call(
        near_kernel,
        (heads(HD, f32), heads(256, f32), state),
        flops=8 * 2 * 256 * 128 * 3000,
        nbytes=8 << 20,
        aliases={5: 0, 6: 1},
    )(swap(own), u1, swap(u1), queries, key_map, m, accl)
    m, accl, st = call(
        wrap_kernel,
        (heads(HD, f32), heads(256, f32), state),
        flops=8 * 2 * 256 * 128 * 1000,
        nbytes=8 << 20,
        aliases={4: 0, 5: 1, 6: 2},
    )(d1, swap(d1), queries, key_map, m, accl, st)
    m, accl, st = call(
        mid_kernel,
        (heads(HD, f32), heads(256, f32), state),
        flops=8 * 2 * 256 * 128 * 3000,
        nbytes=8 << 20,
        aliases={6: 0, 7: 1, 8: 2},
    )(u2, swap(u2), d2, swap(d2), queries, key_map, m, accl, st)
    m, accl, st = call(
        far_kernel,
        (heads(HD, f32), heads(256, f32), state),
        flops=8 * 2 * 256 * 128 * 1500,
        nbytes=8 << 20,
        aliases={4: 0, 5: 1, 6: 2},
    )(x4, swap(x4), queries, key_map, m, accl, st)
    return call(
        last_kernel,
        jax.ShapeDtypeStruct((TOK, 8 * HD), bf16),
        flops=8 * 2 * 256 * 128 * 3000,
        nbytes=8 << 20,
    )(u3, swap(u3), d3, swap(d3), queries, key_map, qf, stu, m, accl, st)


def solution(mesh):
    split = Mesh(mesh.devices.reshape(8, 2, mesh.shape["head"]), ("z", "c", "head"))
    seq = ("z", "c")
    placed = (P(seq, "head"), P(seq, None), P(seq, None), P("head", None, None), P(), P(seq))
    return jax.shard_map(
        per_device, mesh=split, in_specs=placed, out_specs=P(seq, "head"), check_vma=False
    )
```

```python
import math

import jax
import jax.numpy as jnp
from jax import lax
from jax.experimental import pallas as pl
from jax.experimental.pallas import tpu as pltpu
from jax.sharding import Mesh
from jax.sharding import PartitionSpec as P


QHEADS = 128
KVH = 8
LENGTH = 131072
HD = 128
ROWS = 272
TOK = 256
epsilon = 1e-06
masked_score = -1e30
to_exp2 = math.log2(math.e) / math.sqrt(HD)

SWAP = [(0, 1), (1, 0)]


def ring(shift):
    return [(i, (i + shift) % 8) for i in range(8)]


def call(kernel, out_shape, in_specs=None, scratch=(), flops=0, nbytes=0,
         aliases=None):
    more = {} if in_specs is None else {"in_specs": in_specs}
    return pl.pallas_call(
        kernel,
        out_shape=out_shape,
        **more,
        input_output_aliases=aliases or {},
        scratch_shapes=list(scratch),
        compiler_params=pltpu.CompilerParams(vmem_limit_bytes=40 * 1024 * 1024),
        cost_estimate=pl.CostEstimate(
            flops=flops, bytes_accessed=nbytes, transcendentals=0
        ),
    )


def first_group(local_heads):
    return lax.axis_index("head") * local_heads // (QHEADS // KVH)


def pieces(x):
    a = x.astype(jnp.bfloat16)
    x = x - a.astype(jnp.float32)
    b = x.astype(jnp.bfloat16)
    c = (x - b.astype(jnp.float32)).astype(jnp.bfloat16)
    return a.astype(jnp.float32), b.astype(jnp.float32), c.astype(jnp.float32)


def pack_kernel(keys_ref, values_ref, pos_ref, out_ref, pos_vmem, sems):
    g = pl.multiple_of(first_group(8) * HD, HD)
    cp = pltpu.make_async_copy(pos_ref, pos_vmem, sems.at[2])
    ck = pltpu.make_async_copy(keys_ref.at[:, pl.ds(g, HD)], out_ref.at[0:TOK, 0:HD], sems.at[0])
    cv = pltpu.make_async_copy(
        values_ref.at[:, pl.ds(g, HD)], out_ref.at[0:TOK, HD : 2 * HD], sems.at[1]
    )
    cp.start()
    ck.start()
    cv.start()
    cp.wait()
    a = (0.5 * math.pi / LENGTH) * pos_vmem[...].astype(jnp.float32)
    row = lax.broadcasted_iota(jnp.int32, (16, TOK), 0)
    tile = jnp.zeros((16, TOK), jnp.float32)
    for i, part in enumerate(pieces(jnp.cos(a)) + pieces(jnp.sin(a))):
        tile = jnp.where(row == i, part, tile)
    out_ref[TOK:ROWS, :] = tile.astype(jnp.bfloat16)
    ck.wait()
    cv.wait()


def angles_of(block_ref):
    d = block_ref[TOK:ROWS, :].astype(jnp.float32)
    return d[0:1] + d[1:2] + d[2:3], d[3:4] + d[4:5] + d[5:6]


def elu1(x):
    return jnp.where(x > 0.0, x + 1.0, jnp.exp(jnp.minimum(x, 0.0)))


def dot(a, b, dims):
    return lax.dot_general(a, b, (dims, ((), ())), preferred_element_type=jnp.float32)


def nn(a, b):
    return dot(a, b, ((1,), (0,)))


def nt(a, b):
    return dot(a, b, ((1,), (1,)))


def key_feats_t(block_ref, key_map, ok=None):
    c, s = angles_of(block_ref)
    if ok is not None:
        c, s = jnp.where(ok, c, 0.0), jnp.where(ok, s, 0.0)
    phi = elu1(dot(key_map, block_ref[0:TOK, 0:HD], ((0,), (1,))))
    return jnp.concatenate([c * phi, s * phi], axis=0).astype(jnp.bfloat16)


def with_ones(v):
    return jnp.concatenate([v, jnp.ones(v.shape, v.dtype)], axis=1)


def local_kernel(own_ref, q_ref, qmap_ref, kmap_ref, qf_ref, m_ref, accl_ref, stu_ref):
    k = own_ref[0:TOK, 0:HD]
    va = with_ones(own_ref[0:TOK, HD : 2 * HD])
    c, s = angles_of(own_ref)
    ct = jnp.broadcast_to(c, (HD, TOK)).T
    st = jnp.broadcast_to(s, (HD, TOK)).T
    kft = key_feats_t(own_ref, kmap_ref[first_group(8)])
    causal = lax.broadcasted_iota(jnp.int32, (TOK, TOK), 0) >= lax.broadcasted_iota(
        jnp.int32, (TOK, TOK), 1
    )
    for h in range(8):
        q = q_ref[:, h * HD : (h + 1) * HD]
        phi = elu1(nn(q, qmap_ref[h]))
        qf = jnp.concatenate([ct * phi, st * phi], axis=1).astype(jnp.bfloat16)
        qf_ref[h] = qf
        inner = jnp.where(causal, nn(qf, kft), 0.0).astype(jnp.bfloat16)
        stu_ref[h] = nn(inner, va)
        x = jnp.where(causal, nt(q, k), masked_score)
        m = jnp.max(x, axis=1, keepdims=True)
        p = jnp.exp2((x - m) * to_exp2).astype(jnp.bfloat16)
        accl_ref[h] = nn(p, va)
        m_ref[h] = jnp.broadcast_to(m, (TOK, HD))


def scores_of(q_ref, h, blocks):
    q = q_ref[:, h * HD : (h + 1) * HD]
    return [nt(q, b[0:TOK, 0:HD]) for b, _ in blocks]


def softmax_step(xs, blocks, va, m0, accl):
    top = None
    for x, (_, ok) in zip(xs, blocks):
        t = jnp.where(ok, jnp.maximum(x[:, 0:HD], x[:, HD:]), masked_score)
        top = t if top is None else jnp.maximum(top, t)
    top = jnp.max(top, axis=1, keepdims=True)
    m1 = jnp.maximum(m0, jnp.broadcast_to(top, m0.shape))
    f = jnp.exp2((m0 - m1) * to_exp2)
    ps = []
    for x, (_, ok) in zip(xs, blocks):
        mm = jnp.where(ok, m1, -masked_score)
        p = jnp.exp2((x - jnp.concatenate([mm, mm], axis=1)) * to_exp2)
        ps.append(p.astype(jnp.bfloat16))
    add = nn(jnp.concatenate(ps, axis=1), va)
    return m1, accl * jnp.concatenate([f, f], axis=1) + add


def values_of(blocks):
    return jnp.concatenate([with_ones(b[0:TOK, HD : 2 * HD]) for b, _ in blocks], axis=0)


def absorb(blocks, q_ref, kmap_ref, m_from, accl_from, state, m_ref, accl_ref):
    km = kmap_ref[first_group(8)]
    va = values_of(blocks)
    feats = [None] * len(blocks)
    later = scores_of(q_ref, 0, blocks)
    for h in range(8):
        xs = later
        if h < 7:
            later = scores_of(q_ref, h + 1, blocks)
        for i in range(h, len(blocks), 8):
            feats[i] = key_feats_t(blocks[i][0], km, blocks[i][1])
        m_ref[h], accl_ref[h] = softmax_step(xs, blocks, va, m_from[h], accl_from[h])
    return state + nn(jnp.concatenate(feats, axis=1), va)


def near_blocks(pb, u1, u1s):
    z = lax.axis_index("z")
    return [(pb, lax.axis_index("c") == 1), (u1, z >= 1), (u1s, z >= 1)]


def early():
    z = lax.axis_index("z")
    return (z >= 3) & (z < 6)


def near_kernel(pb, u1, u1s, q_ref, kmap_ref, m_in, accl_in, m_ref, accl_ref, state_ref):
    state_ref[...] = jnp.zeros_like(state_ref)

    @pl.when(early())
    def _():
        state_ref[...] = absorb(
            near_blocks(pb, u1, u1s), q_ref, kmap_ref, m_in, accl_in, 0.0, m_ref, accl_ref
        )


def wrap_kernel(pb, u1, u1s, d1, d1s, q_ref, kmap_ref, m_in, accl_in, state_in,
                m_ref, accl_ref, state_ref):
    z = lax.axis_index("z")
    ins = (q_ref, kmap_ref, m_in, accl_in)

    @pl.when(jnp.logical_not(early()))
    def _():
        state_ref[...] = absorb(
            near_blocks(pb, u1, u1s), *ins, state_in[...], m_ref, accl_ref
        )

    @pl.when(z >= 7)
    def _():
        blocks = [(d1, z >= 7), (d1s, z >= 7)]
        state_ref[...] = absorb(
            blocks, q_ref, kmap_ref, m_ref, accl_ref, state_ref[...], m_ref, accl_ref
        )


def mid_kernel(u2, u2s, d2, d2s, q_ref, kmap_ref, m_in, accl_in, state_in,
               m_ref, accl_ref, state_ref):
    z = lax.axis_index("z")
    blocks = [(u2, z >= 2), (u2s, z >= 2)]

    @pl.when((z >= 2) & (z < 6))
    def _():
        state_ref[...] = absorb(
            blocks, q_ref, kmap_ref, m_in, accl_in, state_in[...], m_ref, accl_ref
        )

    @pl.when(z >= 6)
    def _():
        state_ref[...] = absorb(
            blocks + [(d2, z >= 6), (d2s, z >= 6)],
            q_ref, kmap_ref, m_in, accl_in, state_in[...], m_ref, accl_ref,
        )


def far_kernel(x, xs, q_ref, kmap_ref, m_in, accl_in, state_in, m_ref, accl_ref, state_ref):
    z = lax.axis_index("z")

    @pl.when(z >= 4)
    def _():
        state_ref[...] = absorb(
            [(x, z >= 4), (xs, z >= 4)],
            q_ref, kmap_ref, m_in, accl_in, state_in[...], m_ref, accl_ref,
        )


def last_kernel(u3, u3s, d3, d3s, q_ref, kmap_ref, qf_ref, stu_ref, m_in, accl_in, state_in,
                out_ref):
    z = lax.axis_index("z")

    def finish(blocks):
        state = state_in[...]
        if blocks:
            km = kmap_ref[first_group(8)]
            va = values_of(blocks)
            feats = [key_feats_t(b, km, ok) for b, ok in blocks]
            later = scores_of(q_ref, 0, blocks)
            state = state + nn(jnp.concatenate(feats, axis=1), va)
        high = state.astype(jnp.bfloat16)
        for h in range(8):
            accl = accl_in[h]
            if blocks:
                xs = later
                if h < 7:
                    later = scores_of(q_ref, h + 1, blocks)
                _, accl = softmax_step(xs, blocks, va, m_in[h], accl)
            qf = qf_ref[h]
            nd = stu_ref[h] + nn(qf, high)
            student = nd[:, 0:HD] / (nd[:, HD:] + epsilon)
            teacher = (accl[:, 0:HD] / accl[:, HD:]).astype(jnp.bfloat16).astype(jnp.float32)
            out_ref[:, h * HD : (h + 1) * HD] = (2.0 * (student - teacher)).astype(jnp.bfloat16)

    near = [(u3, z >= 3), (u3s, z >= 3)]

    @pl.when(z >= 5)
    def _():
        finish(near + [(d3, z >= 5), (d3s, z >= 5)])

    @pl.when((z >= 3) & (z < 5))
    def _():
        finish(near)

    @pl.when(z < 3)
    def _():
        finish([])


def per_device(queries, keys, values, query_map, key_map, positions):
    f32, bf16 = jnp.float32, jnp.bfloat16
    any_ = pl.BlockSpec(memory_space=pltpu.HBM)
    vm = pl.BlockSpec(memory_space=pltpu.VMEM)
    own = pl.pallas_call(
        pack_kernel,
        out_shape=jax.ShapeDtypeStruct((ROWS, 2 * HD), bf16),
        in_specs=[any_, any_, any_],
        out_specs=vm,
        scratch_shapes=[pltpu.VMEM((1, TOK), jnp.int32), pltpu.SemaphoreType.DMA((3,))],
        name="pack",
        cost_estimate=pl.CostEstimate(flops=4 << 30, bytes_accessed=16 << 20, transcendentals=0),
    )(keys, values, positions.reshape(1, TOK))

    def swap(a):
        return lax.ppermute(a, "c", SWAP)

    def hop(a, shift):
        return lax.ppermute(a, "z", ring(shift))

    u1 = hop(own, 1)
    d1 = hop(own, -1)
    x4 = hop(own, 4)
    u2 = hop(u1, 1)
    d2 = hop(d1, -1)
    u3 = hop(u2, 1)
    d3 = hop(d2, -1)

    heads = lambda w, t: jax.ShapeDtypeStruct((8, TOK, w), t)
    state = jax.ShapeDtypeStruct((2 * HD, 2 * HD), f32)
    qf, m, accl, stu = call(
        local_kernel,
        (
            heads(256, bf16),
            heads(HD, f32),
            heads(256, f32),
            heads(256, f32),
        ),
        flops=8 * 2 * 256 * 128 * 1500,
        nbytes=8 << 20,
    )(own, queries, query_map, key_map)
    near = (swap(own), u1, swap(u1))
    m, accl, st = call(
        near_kernel,
        (heads(HD, f32), heads(256, f32), state),
        flops=8 * 2 * 256 * 128 * 3000,
        nbytes=8 << 20,
        aliases={5: 0, 6: 1},
    )(*near, queries, key_map, m, accl)
    m, accl, st = call(
        wrap_kernel,
        (heads(HD, f32), heads(256, f32), state),
        flops=8 * 2 * 256 * 128 * 1000,
        nbytes=8 << 20,
        aliases={7: 0, 8: 1, 9: 2},
    )(*near, d1, swap(d1), queries, key_map, m, accl, st)
    m, accl, st = call(
        mid_kernel,
        (heads(HD, f32), heads(256, f32), state),
        flops=8 * 2 * 256 * 128 * 3000,
        nbytes=8 << 20,
        aliases={6: 0, 7: 1, 8: 2},
    )(u2, swap(u2), d2, swap(d2), queries, key_map, m, accl, st)
    m, accl, st = call(
        far_kernel,
        (heads(HD, f32), heads(256, f32), state),
        flops=8 * 2 * 256 * 128 * 1500,
        nbytes=8 << 20,
        aliases={4: 0, 5: 1, 6: 2},
    )(x4, swap(x4), queries, key_map, m, accl, st)
    return call(
        last_kernel,
        jax.ShapeDtypeStruct((TOK, 8 * HD), bf16),
        flops=8 * 2 * 256 * 128 * 3000,
        nbytes=8 << 20,
    )(u3, swap(u3), d3, swap(d3), queries, key_map, qf, stu, m, accl, st)


def solution(mesh):
    split = Mesh(mesh.devices.reshape(8, 2, mesh.shape["head"]), ("z", "c", "head"))
    seq = ("z", "c")
    placed = (P(seq, "head"), P(seq, None), P(seq, None), P("head", None, None), P(), P(seq))
    return jax.shard_map(
        per_device, mesh=split, in_specs=placed, out_specs=P(seq, "head"), check_vma=False
    )
```

```python
import math

import jax
import jax.numpy as jnp
from jax import lax
from jax.experimental import pallas as pl
from jax.experimental.pallas import tpu as pltpu
from jax.sharding import Mesh
from jax.sharding import PartitionSpec as P


QHEADS = 128
KVH = 8
LENGTH = 131072
HD = 128
ROWS = 272
TOK = 256
epsilon = 1e-06
masked_score = -1e30
to_exp2 = math.log2(math.e) / math.sqrt(HD)

SWAP = [(0, 1), (1, 0)]


def ring(shift):
    return [(i, (i + shift) % 8) for i in range(8)]


def call(kernel, out_shape, in_specs=None, scratch=(), flops=0, nbytes=0,
         aliases=None):
    more = {} if in_specs is None else {"in_specs": in_specs}
    return pl.pallas_call(
        kernel,
        out_shape=out_shape,
        **more,
        input_output_aliases=aliases or {},
        scratch_shapes=list(scratch),
        compiler_params=pltpu.CompilerParams(vmem_limit_bytes=40 * 1024 * 1024),
        cost_estimate=pl.CostEstimate(
            flops=flops, bytes_accessed=nbytes, transcendentals=0
        ),
    )


def first_group(local_heads):
    return lax.axis_index("head") * local_heads // (QHEADS // KVH)


def pieces(x):
    a = x.astype(jnp.bfloat16)
    x = x - a.astype(jnp.float32)
    b = x.astype(jnp.bfloat16)
    c = (x - b.astype(jnp.float32)).astype(jnp.bfloat16)
    return a.astype(jnp.float32), b.astype(jnp.float32), c.astype(jnp.float32)


def pack_kernel(keys_ref, values_ref, pos_ref, out_ref, pos_vmem, sems):
    g = pl.multiple_of(first_group(8) * HD, HD)
    cp = pltpu.make_async_copy(pos_ref, pos_vmem, sems.at[2])
    ck = pltpu.make_async_copy(keys_ref.at[:, pl.ds(g, HD)], out_ref.at[0:TOK, 0:HD], sems.at[0])
    cv = pltpu.make_async_copy(
        values_ref.at[:, pl.ds(g, HD)], out_ref.at[0:TOK, HD : 2 * HD], sems.at[1]
    )
    cp.start()
    ck.start()
    cv.start()
    cp.wait()
    a = (0.5 * math.pi / LENGTH) * pos_vmem[...].astype(jnp.float32)
    row = lax.broadcasted_iota(jnp.int32, (16, TOK), 0)
    tile = jnp.zeros((16, TOK), jnp.float32)
    for i, part in enumerate(pieces(jnp.cos(a)) + pieces(jnp.sin(a))):
        tile = jnp.where(row == i, part, tile)
    out_ref[TOK:ROWS, :] = tile.astype(jnp.bfloat16)
    ck.wait()
    cv.wait()


def angles_of(block_ref):
    d = block_ref[TOK:ROWS, :].astype(jnp.float32)
    return d[0:1] + d[1:2] + d[2:3], d[3:4] + d[4:5] + d[5:6]


def elu1(x):
    return jnp.where(x > 0.0, x + 1.0, jnp.exp(jnp.minimum(x, 0.0)))


def dot(a, b, dims):
    return lax.dot_general(a, b, (dims, ((), ())), preferred_element_type=jnp.float32)


def nn(a, b):
    return dot(a, b, ((1,), (0,)))


def nt(a, b):
    return dot(a, b, ((1,), (1,)))


def key_feats_t(block_ref, key_map, ok=None):
    c, s = angles_of(block_ref)
    if ok is not None:
        c, s = jnp.where(ok, c, 0.0), jnp.where(ok, s, 0.0)
    phi = elu1(dot(key_map, block_ref[0:TOK, 0:HD], ((0,), (1,))))
    return jnp.concatenate([c * phi, s * phi], axis=0).astype(jnp.bfloat16)


def with_ones(v):
    return jnp.concatenate([v, jnp.ones(v.shape, v.dtype)], axis=1)


def local_kernel(own_ref, q_ref, qmap_ref, kmap_ref, qf_ref, m_ref, accl_ref, stu_ref):
    k = own_ref[0:TOK, 0:HD]
    va = with_ones(own_ref[0:TOK, HD : 2 * HD])
    c, s = angles_of(own_ref)
    ct = jnp.broadcast_to(c, (HD, TOK)).T
    st = jnp.broadcast_to(s, (HD, TOK)).T
    kft = key_feats_t(own_ref, kmap_ref[first_group(8)])
    causal = lax.broadcasted_iota(jnp.int32, (TOK, TOK), 0) >= lax.broadcasted_iota(
        jnp.int32, (TOK, TOK), 1
    )
    for h in range(8):
        q = q_ref[:, h * HD : (h + 1) * HD]
        phi = elu1(nn(q, qmap_ref[h]))
        qf = jnp.concatenate([ct * phi, st * phi], axis=1).astype(jnp.bfloat16)
        qf_ref[h] = qf
        inner = jnp.where(causal, nn(qf, kft), 0.0).astype(jnp.bfloat16)
        stu_ref[h] = nn(inner, va)
        x = jnp.where(causal, nt(q, k), masked_score)
        m = jnp.max(x, axis=1, keepdims=True)
        p = jnp.exp2((x - m) * to_exp2).astype(jnp.bfloat16)
        accl_ref[h] = nn(p, va)
        m_ref[h] = jnp.broadcast_to(m, (TOK, HD))


def scores_of(q_ref, h, blocks):
    q = q_ref[:, h * HD : (h + 1) * HD]
    return [nt(q, b[0:TOK, 0:HD]) for b, _ in blocks]


def softmax_step(xs, blocks, va, m0, accl):
    top = None
    for x, (_, ok) in zip(xs, blocks):
        t = jnp.where(ok, jnp.maximum(x[:, 0:HD], x[:, HD:]), masked_score)
        top = t if top is None else jnp.maximum(top, t)
    top = jnp.max(top, axis=1, keepdims=True)
    m1 = jnp.maximum(m0, jnp.broadcast_to(top, m0.shape))
    f = jnp.exp2((m0 - m1) * to_exp2)
    ps = []
    for x, (_, ok) in zip(xs, blocks):
        mm = jnp.where(ok, m1, -masked_score)
        p = jnp.exp2((x - jnp.concatenate([mm, mm], axis=1)) * to_exp2)
        ps.append(p.astype(jnp.bfloat16))
    add = nn(jnp.concatenate(ps, axis=1), va)
    return m1, accl * jnp.concatenate([f, f], axis=1) + add


def values_of(blocks):
    return jnp.concatenate([with_ones(b[0:TOK, HD : 2 * HD]) for b, _ in blocks], axis=0)


def absorb(blocks, q_ref, kmap_ref, m_from, accl_from, state, m_ref, accl_ref):
    km = kmap_ref[first_group(8)]
    va = values_of(blocks)
    feats = [None] * len(blocks)
    later = scores_of(q_ref, 0, blocks)
    for h in range(8):
        xs = later
        if h < 7:
            later = scores_of(q_ref, h + 1, blocks)
        for i in range(h, len(blocks), 8):
            feats[i] = key_feats_t(blocks[i][0], km, blocks[i][1])
        m_ref[h], accl_ref[h] = softmax_step(xs, blocks, va, m_from[h], accl_from[h])
    return state + nn(jnp.concatenate(feats, axis=1), va)


def near_kernel(pb, u1, u1s, d1, d1s, q_ref, kmap_ref, m_in, accl_in, m_ref, accl_ref, state_ref):
    z = lax.axis_index("z")
    second = lax.axis_index("c") == 1
    ins = (q_ref, kmap_ref, m_in, accl_in)
    outs = (m_ref, accl_ref)

    @pl.when(z == 0)
    def _():
        state_ref[...] = absorb([(pb, second)], *ins, 0.0, *outs)

    @pl.when(z >= 1)
    def _():
        blocks = [(pb, second), (u1, z >= 1), (u1s, z >= 1)]
        state_ref[...] = absorb(blocks, *ins, 0.0, *outs)

    @pl.when(z >= 7)
    def _():
        blocks = [(d1, z >= 7), (d1s, z >= 7)]
        state_ref[...] = absorb(blocks, q_ref, kmap_ref, m_ref, accl_ref, state_ref[...], *outs)


def mid_kernel(u2, u2s, d2, d2s, q_ref, kmap_ref, m_in, accl_in, state_in,
               m_ref, accl_ref, state_ref):
    z = lax.axis_index("z")
    blocks = [(u2, z >= 2), (u2s, z >= 2)]

    @pl.when((z >= 2) & (z < 6))
    def _():
        state_ref[...] = absorb(
            blocks, q_ref, kmap_ref, m_in, accl_in, state_in[...], m_ref, accl_ref
        )

    @pl.when(z >= 6)
    def _():
        state_ref[...] = absorb(
            blocks + [(d2, z >= 6), (d2s, z >= 6)],
            q_ref, kmap_ref, m_in, accl_in, state_in[...], m_ref, accl_ref,
        )


def far_kernel(x, xs, q_ref, kmap_ref, m_in, accl_in, state_in, m_ref, accl_ref, state_ref):
    z = lax.axis_index("z")

    @pl.when(z >= 4)
    def _():
        state_ref[...] = absorb(
            [(x, z >= 4), (xs, z >= 4)],
            q_ref, kmap_ref, m_in, accl_in, state_in[...], m_ref, accl_ref,
        )


def last_kernel(u3, u3s, d3, d3s, q_ref, kmap_ref, qf_ref, stu_ref, m_in, accl_in, state_in,
                out_ref):
    z = lax.axis_index("z")

    def finish(blocks):
        state = state_in[...]
        if blocks:
            km = kmap_ref[first_group(8)]
            va = values_of(blocks)
            feats = [key_feats_t(b, km, ok) for b, ok in blocks]
            later = scores_of(q_ref, 0, blocks)
            state = state + nn(jnp.concatenate(feats, axis=1), va)
        high = state.astype(jnp.bfloat16)
        for h in range(8):
            accl = accl_in[h]
            if blocks:
                xs = later
                if h < 7:
                    later = scores_of(q_ref, h + 1, blocks)
                _, accl = softmax_step(xs, blocks, va, m_in[h], accl)
            qf = qf_ref[h]
            nd = stu_ref[h] + nn(qf, high)
            student = nd[:, 0:HD] / (nd[:, HD:] + epsilon)
            teacher = (accl[:, 0:HD] / accl[:, HD:]).astype(jnp.bfloat16).astype(jnp.float32)
            out_ref[:, h * HD : (h + 1) * HD] = (2.0 * (student - teacher)).astype(jnp.bfloat16)

    near = [(u3, z >= 3), (u3s, z >= 3)]

    @pl.when(z >= 5)
    def _():
        finish(near + [(d3, z >= 5), (d3s, z >= 5)])

    @pl.when((z >= 3) & (z < 5))
    def _():
        finish(near)

    @pl.when(z < 3)
    def _():
        finish([])


def per_device(queries, keys, values, query_map, key_map, positions):
    f32, bf16 = jnp.float32, jnp.bfloat16
    any_ = pl.BlockSpec(memory_space=pltpu.HBM)
    vm = pl.BlockSpec(memory_space=pltpu.VMEM)
    own = pl.pallas_call(
        pack_kernel,
        out_shape=jax.ShapeDtypeStruct((ROWS, 2 * HD), bf16),
        in_specs=[any_, any_, any_],
        out_specs=vm,
        scratch_shapes=[pltpu.VMEM((1, TOK), jnp.int32), pltpu.SemaphoreType.DMA((3,))],
        name="pack",
        cost_estimate=pl.CostEstimate(flops=4 << 30, bytes_accessed=16 << 20, transcendentals=0),
    )(keys, values, positions.reshape(1, TOK))

    def swap(a):
        return lax.ppermute(a, "c", SWAP)

    def hop(a, shift):
        return lax.ppermute(a, "z", ring(shift))

    u1 = hop(own, 1)
    d1 = hop(own, -1)
    x4 = hop(own, 4)
    u2 = hop(u1, 1)
    d2 = hop(d1, -1)
    u3 = hop(u2, 1)
    d3 = hop(d2, -1)

    heads = lambda w, t: jax.ShapeDtypeStruct((8, TOK, w), t)
    state = jax.ShapeDtypeStruct((2 * HD, 2 * HD), f32)
    qf, m, accl, stu = call(
        local_kernel,
        (
            heads(256, bf16),
            heads(HD, f32),
            heads(256, f32),
            heads(256, f32),
        ),
        flops=8 * 2 * 256 * 128 * 1500,
        nbytes=8 << 20,
    )(own, queries, query_map, key_map)
    m, accl, st = call(
        near_kernel,
        (heads(HD, f32), heads(256, f32), state),
        flops=8 * 2 * 256 * 128 * 3000,
        nbytes=8 << 20,
        aliases={7: 0, 8: 1},
    )(swap(own), u1, swap(u1), d1, swap(d1), queries, key_map, m, accl)
    m, accl, st = call(
        mid_kernel,
        (heads(HD, f32), heads(256, f32), state),
        flops=8 * 2 * 256 * 128 * 3000,
        nbytes=8 << 20,
        aliases={6: 0, 7: 1, 8: 2},
    )(u2, swap(u2), d2, swap(d2), queries, key_map, m, accl, st)
    m, accl, st = call(
        far_kernel,
        (heads(HD, f32), heads(256, f32), state),
        flops=8 * 2 * 256 * 128 * 1500,
        nbytes=8 << 20,
        aliases={4: 0, 5: 1, 6: 2},
    )(x4, swap(x4), queries, key_map, m, accl, st)
    return call(
        last_kernel,
        jax.ShapeDtypeStruct((TOK, 8 * HD), bf16),
        flops=8 * 2 * 256 * 128 * 3000,
        nbytes=8 << 20,
    )(u3, swap(u3), d3, swap(d3), queries, key_map, qf, stu, m, accl, st)


def solution(mesh):
    split = Mesh(mesh.devices.reshape(8, 2, mesh.shape["head"]), ("z", "c", "head"))
    seq = ("z", "c")
    placed = (P(seq, "head"), P(seq, None), P(seq, None), P("head", None, None), P(), P(seq))
    return jax.shard_map(
        per_device, mesh=split, in_specs=placed, out_specs=P(seq, "head"), check_vma=False
    )
```
